32 devices in a mesh: grp: 2 (over y), sink: 16 (over z, x, core).
Axes of the slice: x: 2, y: 2, z: 4, core: 2. Of those that a mesh axis runs over, the one named last changes fastest.
Arguments:
- meson: float32 [32, 2, 256, 256], P(('grp', 'sink')), parts along dimension 0, may hold values from -0.25 to 0.25
- meson_src: float32 [8192, 256], P(('grp', 'sink')), parts along dimension 0, may hold values from -0.25 to 0.25
- peram: float32 [32, 8, 2, 256, 256], P(('grp', 'sink')), parts along dimension 0, may hold values from -0.375 to 0.375
- pair_left: int32 [32, 16], P(('grp', 'sink')), parts along dimension 0, may hold values from 0 to 7
- pair_right: int32 [32, 16], P(('grp', 'sink')), parts along dimension 0, may hold values from 0 to 7
- pair_weight: int32 [32, 16], P(('grp', 'sink')), parts along dimension 0, may hold values from -2 to 2
- pair_count: int32 [32], P(('grp', 'sink')), parts along dimension 0, may hold values from 1 to 16, 136 in all
Outputs:
- two_meson: float32 [32, 2, 256, 256], P(('grp', 'sink')), parts along dimension 0
The draws below stay inside these ranges and needn't reach their ends.
There are 2 independent parts, one for each index of `grp`. The reference program is written for one: setup_inputs(seed, part) draws one part's arguments, and reference() takes and returns one part's arrays. A program takes and returns all parts, laid end to end along the dimension named above; each array names one. Nothing has to cross between parts.
Inputs may be any that keep to these rules, and one draw needn't show every extreme that they name: `pair_count`: each sink time's count is at least 1 and some sink time has exactly 16; entries past the count are ignored.
All inputs are finite; a program needn't handle non-finite values. No bound on the sum of `pair_count` on one device may be relied on, other than what follows from the above.
Results may differ from the reference program's by a relative error of at most 0.0003.
Values sent between devices are 32-bit elements; how exact they have to be, the bound alone decides.
No kernel may reach another device: no remote copies, remote signals or barrier semaphores. Data moves between devices by JAX's collectives and lax.ppermute only.
A program may use at most 64 MiB of HBM per device.

```python
import math
from functools import partial
import jax
import jax.numpy as jnp
import numpy as np
from jax import lax

NVEC = 256
NSRC = 8
NPAIR = 16
NT = 16
PAIR_TOTAL = 136


def with_ends(result, key, least, top_value):
    spot = [jax.random.randint(jax.random.fold_in(key, axis), (), 0, length) for axis, length in enumerate(result.shape)]
    longest = result.shape.index(max(result.shape))
    next_to = spot[:longest] + [(spot[longest] + 1) % result.shape[longest]] + spot[longest + 1:]
    return result.at[tuple(spot)].set(least).at[tuple(next_to)].set(top_value)


def block_scale(own_key, dims, pieces, low, top_value):
    factor_of, own = 1.0, jax.random.fold_in(own_key, 6)
    for position, shards_of in pieces:
        steps = jnp.exp(jax.random.uniform(jax.random.fold_in(own, position), (shards_of,), jnp.float32, low / len(pieces), top_value / len(pieces)))
        factor_of = factor_of * jnp.repeat(steps, dims[position] // shards_of).reshape([-1 if axis == position else 1 for axis in range(len(dims))])
    return factor_of


def profile(amount, total, limit, slope):
    loads = [(1 << 20) // math.isqrt(standing ** slope) + 1 for standing in range(2, amount + 1)]
    surplus, counts = total - limit - (amount - 1), [1] * (amount - 1)
    while surplus > 0:
        candidates = [i for i in range(amount - 1) if counts[i] < limit]
        mass, remaining = sum([loads[i] for i in candidates]), surplus
        for i in candidates:
            addition = min(limit - counts[i], max(1, remaining * loads[i] // mass), surplus)
            counts[i] = counts[i] + addition
            surplus = surplus - addition
    return np.array([limit] + counts)


def uneven(stream_key, number_of, total, reach, lean):
    if number_of == 2:
        one = jax.random.randint(stream_key, (), max(1, total - reach), min(reach, total - 1) + 1)
        return jnp.stack([one, total - one])
    lengths = jnp.asarray(profile(number_of, total, reach, lean), jnp.int32)
    pairs = (number_of - 1) // 2
    donor, receiver = lengths[1:1 + 2 * pairs:2], lengths[2:2 + 2 * pairs:2]
    slack = jnp.minimum(donor - 1, reach - receiver)
    passed = jax.random.randint(jax.random.fold_in(stream_key, 1), (pairs,), 0, 1 << 20) % (slack + 1)
    lengths = lengths.at[1:1 + 2 * pairs:2].set(donor - passed).at[2:2 + 2 * pairs:2].set(receiver + passed)
    return lengths[jax.random.permutation(jax.random.fold_in(stream_key, 2), number_of)]


def noise(rng, extent, scale, bound, cuts=(), kind=jnp.bfloat16):
    drawn = scale * jax.random.normal(rng, extent, jnp.float32)
    if cuts:
        drawn = drawn * block_scale(rng, extent, cuts, -0.22, 0.18)
    return jnp.clip(drawn, -bound, bound).astype(kind)


def setup_inputs(seed: int = 0, part: int = 0) -> dict:
    streams_of = jax.random.split(jax.random.key(seed), 8)
    own_keys = jax.random.split(jax.random.fold_in(streams_of[7], part), 8)
    return {
        "meson": noise(own_keys[0], (NT, 2, NVEC, NVEC), (2 * NVEC) ** -0.5, 0.25, ((0, 16),), jnp.float32),
        "meson_src": noise(own_keys[1], (NSRC * 2 * NVEC, NVEC), (2 * NVEC) ** -0.5, 0.25, ((0, 16),), jnp.float32),
        "peram": noise(own_keys[2], (NT, NSRC, 2, NVEC, NVEC), NVEC ** -0.5, 0.375, ((0, 16),), jnp.float32),
        "pair_left": with_ends(jax.random.randint(own_keys[3], (NT, NPAIR), 0, NSRC), jax.random.fold_in(own_keys[3], 1), 0, NSRC - 1).astype(jnp.int32),
        "pair_right": with_ends(jax.random.randint(own_keys[4], (NT, NPAIR), 0, NSRC), jax.random.fold_in(own_keys[4], 1), 0, NSRC - 1).astype(jnp.int32),
        "pair_weight": with_ends(jax.random.randint(own_keys[5], (NT, NPAIR), -2, 3), jax.random.fold_in(own_keys[5], 1), -2, 2).astype(jnp.int32),
        "pair_count": uneven(own_keys[6], NT, PAIR_TOTAL, NPAIR, 2).astype(jnp.int32),
    }


def complex_product(pattern, left_real, left_imag, right_real, right_imag):
    contract = partial(jnp.einsum, pattern, precision=lax.Precision.HIGHEST)
    return (contract(left_real, right_real) - contract(left_imag, right_imag),
            contract(left_real, right_imag) + contract(left_imag, right_real))


def node_blocks(meson_slice, perams, source_real, source_imag):
    contract = partial(jnp.einsum, "sab,scb->sac", precision=lax.Precision.HIGHEST)
    tau_real = perams[:, 0]
    tau_imag = perams[:, 1]
    hold_real = contract(source_real, tau_real) + contract(source_imag, tau_imag)
    hold_imag = contract(source_imag, tau_real) - contract(source_real, tau_imag)
    front_real, front_imag = complex_product("ab,sbc->sac", meson_slice[0], meson_slice[1], tau_real, tau_imag)
    return complex_product("sab,sbc->sac", front_real, front_imag, hold_real, hold_imag)


def weight_table(left_list, right_list, weight_list, count, sources):
    slots = left_list.shape[0]
    live = jnp.arange(slots, dtype=jnp.int32) < count
    scaled = jnp.where(live, weight_list, 0).astype(jnp.float32)
    labels = jnp.arange(sources, dtype=jnp.int32)
    left_table = (left_list[:, None] == labels[None, :]).astype(jnp.float32) * scaled[:, None]
    right_table = (right_list[:, None] == labels[None, :]).astype(jnp.float32)
    return jnp.dot(left_table.T, right_table, precision=lax.Precision.HIGHEST)


def table_sum(table, left_pair, right_pair):
    mixing = partial(jnp.einsum, "ij,jab->iab", precision=lax.Precision.HIGHEST)
    mixed_real = mixing(table, right_pair[0])
    mixed_imag = mixing(table, right_pair[1])
    return jnp.stack(complex_product("iab,ibc->ac", left_pair[0], left_pair[1], mixed_real, mixed_imag))


def reference(meson, meson_src, peram, pair_left, pair_right, pair_weight, pair_count):
    source = meson_src.reshape(NSRC, 2, NVEC, NVEC)

    def one_time(items):
        return jnp.stack(node_blocks(items[0], items[1], source[:, 0], source[:, 1]))

    blocks = lax.map(one_time, (meson, peram))
    partner = (jnp.arange(NT, dtype=jnp.int32) + NT // 2) % NT
    partner_blocks = blocks[partner]

    def one_sum(items):
        own, other, left_list, right_list, weight_list, count = items
        table = weight_table(left_list, right_list, weight_list, count, NSRC)
        return table_sum(table, (own[0], own[1]), (other[0], other[1]))

    return lax.map(one_sum, (blocks, partner_blocks, pair_left, pair_right, pair_weight, pair_count))
```

```python
from functools import partial

import jax
import jax.numpy as jnp
from jax import lax
from jax.sharding import PartitionSpec as P

HIGH = lax.Precision.HIGH


def swapped(value, axis, mask):
    pairs = [(source, source ^ mask) for source in range(lax.axis_size(axis))]
    return lax.ppermute(value, axis, pairs)


def sent(value, axis, mask, senders):
    return lax.ppermute(value, axis, [(source, source ^ mask) for source in senders])


def complex_product(pattern, left, right):
    contract = partial(jnp.einsum, pattern, precision=HIGH)
    return (
        contract(left[0], right[0]) - contract(left[1], right[1]),
        contract(left[0], right[1]) + contract(left[1], right[0]),
    )


def joined(shards, axis, me, group):
    for bit in range(group.bit_length() - 1):
        other = swapped(shards, axis, 1 << bit)
        upper = ((me >> bit) & 1) == 1
        low = jnp.where(upper, other, shards)
        high = jnp.where(upper, shards, other)
        shards = jnp.concatenate([low, high], axis=1)
    return shards


def table_of(left_list, right_list, weight_list, count, left_labels, right_labels):
    live = jnp.arange(left_list.shape[0], dtype=jnp.int32) < count
    scaled = jnp.where(live, weight_list, 0).astype(jnp.float32)
    left = (left_list[:, None] == left_labels[None, :]).astype(jnp.float32) * scaled[:, None]
    right = (right_list[:, None] == right_labels[None, :]).astype(jnp.float32)
    return jnp.dot(left.T, right, precision=lax.Precision.HIGHEST)


def body(meson, meson_src, peram, pair_left, pair_right, pair_weight, pair_count):
    axis = "sink"
    n = lax.axis_size(axis)
    sources, width = peram.shape[1], peram.shape[3]
    group, half = n // sources, n // 2
    me = lax.axis_index(axis)
    senders = [d for d in range(n) if (d & 1) == d // half]
    receivers = [d ^ half for d in senders]
    is_sender = (me & 1) == me // half
    mine = me // group

    own = meson_src[None]
    far = swapped(own, axis, half)
    w0 = own
    s0 = joined(w0, axis, me, group)
    w1 = swapped(w0, axis, group)
    s1 = joined(w1, axis, me, group)
    w23 = swapped(jnp.concatenate([w0, w1]), axis, 2 * group)
    s23 = joined(w23, axis, me, group)
    w4 = far
    w5 = swapped(w4, axis, group)
    w45 = jnp.concatenate([w4, w5])
    s45 = joined(w45, axis, me, group)
    w67 = swapped(w45, axis, 2 * group)
    s67 = joined(w67, axis, me, group)

    lists = jnp.stack([pair_left[0], pair_right[0], pair_weight[0]]).astype(jnp.float32)
    lists = jnp.concatenate([lists, jnp.full_like(lists[:1], pair_count[0].astype(jnp.float32))])
    other_lists = swapped(lists, axis, half).astype(jnp.int32)

    def blocks_of(first, source):
        size = source.shape[0]
        source = source.reshape(size, 2, width, width)
        tau = jnp.stack(
            [
                lax.dynamic_index_in_dim(peram[0], mine ^ (first + i), 0, keepdims=False)
                for i in range(size)
            ]
        )
        contract = partial(jnp.einsum, "sab,scb->sac", precision=HIGH)
        sr, si, tr, ti = source[:, 0], source[:, 1], tau[:, 0], tau[:, 1]
        hold = (contract(sr, tr) + contract(si, ti), contract(si, tr) - contract(sr, ti))
        front = complex_product("ab,sbc->sac", (meson[0, 0], meson[0, 1]), (tr, ti))
        return jnp.stack(complex_product("sab,sbc->sac", front, hold))

    parts, arrived = [], []
    first = 0
    for source in (s0, s1, s23, s45, s67):
        part = blocks_of(first, source)
        parts.append(part)
        arrived.append((first, sent(part, axis, half, senders)))
        first += source.shape[0]
    blocks = jnp.concatenate(parts, axis=1)

    here = mine ^ jnp.arange(sources, dtype=jnp.int32)
    there = here ^ (sources // 2)
    own_table = table_of(
        pair_left[0], pair_right[0], pair_weight[0], pair_count[0], here, there
    )
    other_table = table_of(
        other_lists[0], other_lists[1], other_lists[2], other_lists[3, 0], there, here
    )
    left = jnp.einsum("ij,ciab->cjab", own_table, blocks, precision=HIGH)
    right = jnp.einsum("ij,cjab->ciab", other_table, blocks, precision=HIGH)
    result, back = 0.0, 0.0
    for first, block in arrived:
        span = slice(first, first + block.shape[1])
        block = (block[0], block[1])
        result += jnp.stack(
            complex_product("sab,sbc->ac", (left[0, span], left[1, span]), block)
        )
        back += jnp.stack(
            complex_product("sab,sbc->ac", block, (right[0, span], right[1, span]))
        )
    returned = sent(back, axis, half, receivers)
    return jnp.where(is_sender, returned, result)[None]


def solution(mesh):
    placed = (
        P(("grp", "sink"), None, None, None),
        P(("grp", "sink"), None),
        P(("grp", "sink"), None, None, None, None),
        P(("grp", "sink"), None),
        P(("grp", "sink"), None),
        P(("grp", "sink"), None),
        P(("grp", "sink")),
    )
    return jax.shard_map(
        body,
        mesh=mesh,
        in_specs=placed,
        out_specs=P(("grp", "sink"), None, None, None),
        check_vma=False,
    )
```

```python
from functools import partial

import jax
import jax.numpy as jnp
from jax import lax
from jax.experimental import pallas as pl
from jax.experimental.pallas import tpu as pltpu
from jax.sharding import PartitionSpec as P

F32 = jnp.float32
NN = (((1,), (0,)), ((), ()))
NT = (((1,), (1,)), ((), ()))
ROWS = (64, 64, 64, 64)


def swapped(value, axis, mask):
    pairs = [(source, source ^ mask) for source in range(lax.axis_size(axis))]
    return lax.ppermute(value, axis, pairs)


def sent(value, axis, mask, senders):
    return lax.ppermute(value, axis, [(source, source ^ mask) for source in senders])


def halves(value):
    high = value.astype(jnp.bfloat16)
    return high, (value - high.astype(F32)).astype(jnp.bfloat16)


def product(left, right, adjoint=False):
    (rh, rl), (ih, il) = halves(left[0]), halves(left[1])
    left_terms = jnp.concatenate([rh, ih, rh, ih, rl, il], axis=1)
    (rh, rl), (ih, il) = halves(right[0]), halves(right[1])
    if adjoint:
        real = jnp.concatenate([rh, ih, rl, il, rh, ih], axis=1)
        imag = jnp.concatenate([-ih, rh, -il, rl, -ih, rh], axis=1)
    else:
        real = jnp.concatenate([rh, -ih, rl, -il, rh, -ih], axis=0)
        imag = jnp.concatenate([ih, rh, il, rl, ih, rh], axis=0)
    dot = partial(
        lax.dot_general,
        left_terms,
        dimension_numbers=NT if adjoint else NN,
        preferred_element_type=F32,
    )
    return dot(real), dot(imag)


def block_kernel(spans, place, meson, tau, first, second, *refs):
    chunks, blocks = refs[-1 - len(spans) : -1], refs[-1]
    odd = place[1] == 1
    one, two = first[0], second[0]
    source = (jnp.where(odd, two, one), jnp.where(odd, one, two))
    wave = (tau[0, 0, 0], tau[0, 0, 1])
    hold = product(source, wave, adjoint=True)
    front = product((meson[0, 0], meson[0, 1]), wave)
    block = product(front, hold)
    for part in range(2):
        blocks[0, part] = block[part]
        for (low, size), chunk in zip(spans, chunks, strict=True):
            chunk[0, part] = block[part][low : low + size]


def blocks_of(place, meson, peram, first, second, blocks, start, spans):
    size, width = first.shape[0], first.shape[-1]
    sources = peram.shape[1]
    whole = (1, 2, width, width)
    in_specs = [
        pl.BlockSpec(whole, lambda i, p: (0, 0, 0, 0)),
        pl.BlockSpec((1,) + whole, lambda i, p: (0, p[0] ^ (start + i), 0, 0, 0)),
        pl.BlockSpec((1, width, width), lambda i, p: (i, 0, 0)),
        pl.BlockSpec((1, width, width), lambda i, p: (i, 0, 0)),
    ]
    operands = [meson, peram, first, second]
    aliases = {}
    if blocks is not None:
        in_specs.append(pl.BlockSpec(memory_space=pl.ANY))
        operands.append(blocks)
        aliases = {len(operands): len(spans)}
    shapes = [jax.ShapeDtypeStruct((size, 2, rows, width), F32) for _, rows in spans]
    shapes.append(jax.ShapeDtypeStruct((sources, 2, width, width), F32))
    out_specs = [pl.BlockSpec((1, 2, rows, width), lambda i, p: (i, 0, 0, 0)) for _, rows in spans]
    out_specs.append(pl.BlockSpec(whole, lambda i, p: (start + i, 0, 0, 0)))
    outs = pl.pallas_call(
        partial(block_kernel, spans),
        out_shape=shapes,
        grid_spec=pltpu.PrefetchScalarGridSpec(
            num_scalar_prefetch=1, grid=(size,), in_specs=in_specs, out_specs=out_specs
        ),
        input_output_aliases=aliases,
        cost_estimate=pl.CostEstimate(
            flops=size * 72 * width**3, bytes_accessed=size * 28 * width**2, transcendentals=0
        ),
        name="blocks",
    )(place, *operands)
    return outs[:-1], outs[-1]


def mix_kernel(own_list, other_list, place, blocks, left, right):
    left[...] = jnp.zeros_like(left)
    right[...] = jnp.zeros_like(right)
    here, there = place[0], place[2]

    def own(e, _):
        weight = own_list[2, e].astype(F32)
        left[own_list[1, e] ^ there] += weight * blocks[own_list[0, e] ^ here]
        return 0

    def other(e, _):
        weight = other_list[2, e].astype(F32)
        right[other_list[0, e] ^ there] += weight * blocks[other_list[1, e] ^ here]
        return 0

    lax.fori_loop(0, own_list[3, 0], own, 0)
    lax.fori_loop(0, other_list[3, 0], other, 0)


def mixed(own_list, other_list, place, blocks):
    smem, vmem = pl.BlockSpec(memory_space=pltpu.SMEM), pl.BlockSpec(memory_space=pltpu.VMEM)
    shape = jax.ShapeDtypeStruct(blocks.shape, F32)
    return pl.pallas_call(
        mix_kernel,
        out_shape=(shape, shape),
        in_specs=[smem, smem, smem, vmem],
        out_specs=(vmem, vmem),
        cost_estimate=pl.CostEstimate(
            flops=blocks.size * 4, bytes_accessed=blocks.size * 12, transcendentals=0
        ),
        name="mix",
    )(own_list, other_list, place, blocks)


def finish_kernel(chunk, left, right, *refs):
    result, back = refs[-2:]
    block = (chunk[0, 0], chunk[0, 1])
    forth = product((left[0, 0], left[0, 1]), block)
    home = product(block, (right[0, 0], right[0, 1]))

    @pl.when(pl.program_id(0) == 0)
    def _():
        for part in range(2):
            if len(refs) == 4:
                result[part] = refs[0][part]
                back[part] = refs[1][part]
            else:
                result[part] = jnp.zeros_like(result[part])
                back[part] = jnp.zeros_like(back[part])

    for part in range(2):
        result[part] += forth[part]
        back[part] += home[part]


def finished(chunk, left, right, start, sums):
    size, width = chunk.shape[0], chunk.shape[-1]
    whole = (1, 2, width, width)
    total = pl.BlockSpec((2, width, width), lambda i: (0, 0, 0))
    shape = jax.ShapeDtypeStruct((2, width, width), F32)
    return pl.pallas_call(
        finish_kernel,
        out_shape=(shape, shape),
        grid=(size,),
        in_specs=[
            pl.BlockSpec(whole, lambda i: (i, 0, 0, 0)),
            pl.BlockSpec(whole, lambda i: (start + i, 0, 0, 0)),
            pl.BlockSpec(whole, lambda i: (start + i, 0, 0, 0)),
        ]
        + [total] * len(sums),
        out_specs=(total, total),
        cost_estimate=pl.CostEstimate(
            flops=size * 48 * width**3, bytes_accessed=size * 24 * width**2, transcendentals=0
        ),
        name="finish",
    )(chunk, left, right, *sums)


def back_kernel(low, size, chunk, right, back, out):
    real, imag = back[0, low : low + size], back[1, low : low + size]
    for k in range(chunk.shape[0]):
        more = product((chunk[k, 0], chunk[k, 1]), (right[k, 0], right[k, 1]))
        real += more[0]
        imag += more[1]
    out[0], out[1] = real, imag


def rows_back(chunk, right, start, back, low):
    size, _, rows, width = chunk.shape
    return pl.pallas_call(
        partial(back_kernel, low, rows),
        out_shape=jax.ShapeDtypeStruct((2, rows, width), F32),
        grid=(1,),
        in_specs=[
            pl.BlockSpec(chunk.shape, lambda i: (0, 0, 0, 0)),
            pl.BlockSpec((size, 2, width, width), lambda i: (start // size, 0, 0, 0)),
            pl.BlockSpec(back.shape, lambda i: (0, 0, 0)),
        ],
        out_specs=pl.BlockSpec((2, rows, width), lambda i: (0, 0, 0)),
        cost_estimate=pl.CostEstimate(
            flops=size * 24 * rows * width**2, bytes_accessed=12 * width**2, transcendentals=0
        ),
        name="rows_back",
    )(chunk, right, back)


def last_kernel(spans, left, result, *refs):
    chunks, out = refs[:-1], refs[-1]
    real, imag = result[0], result[1]
    for k in range(left.shape[0]):
        block = tuple(jnp.concatenate([chunk[k, part] for chunk in chunks]) for part in range(2))
        more = product((left[k, 0], left[k, 1]), block)
        real += more[0]
        imag += more[1]
    out[0], out[1] = real, imag


def last_added(chunks, left, start, result, spans):
    size, width = chunks[0].shape[0], chunks[0].shape[-1]
    return pl.pallas_call(
        partial(last_kernel, spans),
        out_shape=jax.ShapeDtypeStruct(result.shape, F32),
        grid=(1,),
        in_specs=[
            pl.BlockSpec((size, 2, width, width), lambda i: (start // size, 0, 0, 0)),
            pl.BlockSpec(result.shape, lambda i: (0, 0, 0)),
        ]
        + [pl.BlockSpec(chunk.shape, lambda i: (0, 0, 0, 0)) for chunk in chunks],
        out_specs=pl.BlockSpec(result.shape, lambda i: (0, 0, 0)),
        cost_estimate=pl.CostEstimate(
            flops=size * 24 * width**3, bytes_accessed=24 * width**2, transcendentals=0
        ),
        name="last",
    )(left, result, *chunks)


def body(meson, meson_src, peram, pair_left, pair_right, pair_weight, pair_count):
    axis = "sink"
    n = lax.axis_size(axis)
    sources, width = peram.shape[1], peram.shape[3]
    group, half = n // sources, n // 2
    me = lax.axis_index(axis)
    senders = [d for d in range(n) if (d & 1) == d // half]
    receivers = [d ^ half for d in senders]
    is_sender = (me & 1) == me // half
    mine = me // group

    def whole(shards):
        if group == 2:
            return shards, swapped(shards, axis, 1)
        for bit in range(group.bit_length() - 1):
            other = swapped(shards, axis, 1 << bit)
            upper = ((me >> bit) & 1) == 1
            low, high = jnp.where(upper, other, shards), jnp.where(upper, shards, other)
            shards = jnp.concatenate([low, high], axis=1)
        return shards[:, :width], shards[:, width:]

    odd = me & 1 if group == 2 else 0
    place = jnp.stack([mine, odd, mine ^ (sources // 2)]).astype(jnp.int32)
    count = jnp.broadcast_to(pair_count[:, None], pair_left.shape)
    own_list = jnp.concatenate([pair_left, pair_right, pair_weight, count])

    w0 = meson_src[None]
    s0 = whole(w0)
    w4 = swapped(w0, axis, half)
    w1 = swapped(w0, axis, group)
    s1 = whole(w1)
    w23 = swapped(jnp.concatenate([w0, w1]), axis, 2 * group)
    s23 = whole(w23)
    w45 = jnp.concatenate([w4, swapped(w4, axis, group)])
    s45 = whole(w45)
    s67 = whole(swapped(w45, axis, 2 * group))
    other_list = swapped(own_list, axis, half)

    lows = [sum(ROWS[:r]) * width // 256 for r in range(len(ROWS))]
    spans = [(low, rows * width // 256) for low, rows in zip(lows, ROWS, strict=True)]
    blocks, arrived, start = None, [], 0
    for source in (s0, s1, s23, s45):
        (chunk,), blocks = blocks_of(place, meson, peram, *source, blocks, start, [(0, width)])
        arrived.append((start, sent(chunk, axis, half, senders)))
        start += source[0].shape[0]
    chunks, blocks = blocks_of(place, meson, peram, *s67, blocks, start, spans)
    chunks = [sent(chunk, axis, half, senders) for chunk in chunks]

    left, right = mixed(own_list, other_list, place, blocks)
    sums = ()
    for at, chunk in arrived:
        sums = finished(chunk, left, right, at, sums)
    result, back = sums
    returned = [
        sent(rows_back(chunk, right, start, back, low), axis, half, receivers)
        for chunk, (low, _) in zip(chunks, spans, strict=True)
    ]
    result = last_added(chunks, left, start, result, spans)
    return jnp.where(is_sender, jnp.concatenate(returned, axis=1), result)[None]


def solution(mesh):
    placed = (
        P(("grp", "sink"), None, None, None),
        P(("grp", "sink"), None),
        P(("grp", "sink"), None, None, None, None),
        P(("grp", "sink"), None),
        P(("grp", "sink"), None),
        P(("grp", "sink"), None),
        P(("grp", "sink")),
    )
    return jax.shard_map(
        body,
        mesh=mesh,
        in_specs=placed,
        out_specs=P(("grp", "sink"), None, None, None),
        check_vma=False,
    )
```

```python
from functools import partial

import jax
import jax.numpy as jnp
from jax import lax
from jax.experimental import pallas as pl
from jax.experimental.pallas import tpu as pltpu
from jax.sharding import PartitionSpec as P


F32 = jnp.float32
VMEM = 24 << 20
NN = (((1,), (0,)), ((), ()))
NT = (((1,), (1,)), ((), ()))
ROWS = (64, 64, 64, 64)


def sent(value, axis, mask, senders):
    return lax.ppermute(value, axis, [(source, source ^ mask) for source in senders])


def swapped(value, axis, mask):
    return sent(value, axis, mask, range(lax.axis_size(axis)))


def halves(value):
    high = value.astype(jnp.bfloat16)
    return high, (value - high.astype(F32)).astype(jnp.bfloat16)


def product(left, right, adjoint=False):
    (rh, rl), (ih, il) = halves(left[0]), halves(left[1])
    left_terms = jnp.concatenate([rh, ih, rh, ih, rl, il], axis=1)
    (rh, rl), (ih, il) = halves(right[0]), halves(right[1])
    if adjoint:
        real = jnp.concatenate([rh, ih, rl, il, rh, ih], axis=1)
        imag = jnp.concatenate([-ih, rh, -il, rl, -ih, rh], axis=1)
    else:
        real = jnp.concatenate([rh, -ih, rl, -il, rh, -ih], axis=0)
        imag = jnp.concatenate([ih, rh, il, rl, ih, rh], axis=0)
    dot = partial(
        lax.dot_general,
        left_terms,
        dimension_numbers=NT if adjoint else NN,
        preferred_element_type=F32,
    )
    return dot(real), dot(imag)


def block_kernel(spans, place, meson, tau, first, second, *refs):
    chunks, blocks = refs[-1 - len(spans) : -1], refs[-1]
    odd = place[1] == 1
    one, two = first[0], second[0]
    source = (jnp.where(odd, two, one), jnp.where(odd, one, two))
    wave = (tau[0, 0, 0], tau[0, 0, 1])
    hold = product(source, wave, adjoint=True)
    front = product((meson[0, 0], meson[0, 1]), wave)
    block = product(front, hold)
    for part in range(2):
        blocks[0, part] = block[part]
        for (low, size), chunk in zip(spans, chunks, strict=True):
            chunk[0, part] = block[part][low : low + size]


def blocks_of(place, meson, peram, first, second, blocks, start, spans):
    size, width = first.shape[0], first.shape[-1]
    sources = peram.shape[1]
    whole = (1, 2, width, width)
    in_specs = [
        pl.BlockSpec(whole, lambda i, p: (0, 0, 0, 0)),
        pl.BlockSpec((1,) + whole, lambda i, p: (0, p[0] ^ (start + i), 0, 0, 0)),
        pl.BlockSpec((1, width, width), lambda i, p: (i, 0, 0)),
        pl.BlockSpec((1, width, width), lambda i, p: (i, 0, 0)),
    ]
    operands = [meson, peram, first, second]
    aliases = {}
    if blocks is not None:
        in_specs.append(pl.BlockSpec(memory_space=pl.ANY))
        operands.append(blocks)
        aliases = {len(operands): len(spans)}
    shapes = [jax.ShapeDtypeStruct((size, 2, rows, width), F32) for _, rows in spans]
    shapes.append(jax.ShapeDtypeStruct((sources, 2, width, width), F32))
    out_specs = [pl.BlockSpec((1, 2, rows, width), lambda i, p: (i, 0, 0, 0)) for _, rows in spans]
    out_specs.append(pl.BlockSpec(whole, lambda i, p: (start + i, 0, 0, 0)))
    outs = pl.pallas_call(
        partial(block_kernel, spans),
        out_shape=shapes,
        grid_spec=pltpu.PrefetchScalarGridSpec(
            num_scalar_prefetch=1, grid=(size,), in_specs=in_specs, out_specs=out_specs
        ),
        input_output_aliases=aliases,
        cost_estimate=pl.CostEstimate(
            flops=size * 72 * width**3, bytes_accessed=size * 28 * width**2, transcendentals=0
        ),
        compiler_params=pltpu.CompilerParams(vmem_limit_bytes=VMEM),
        name="blocks",
    )(place, *operands)
    return outs[:-1], outs[-1]


def mix_kernel(own_list, other_list, place, blocks, left, right):
    left[...] = jnp.zeros_like(left)
    right[...] = jnp.zeros_like(right)
    here, there = place[0], place[2]

    def own(e, _):
        weight = own_list[2, e].astype(F32)
        left[own_list[1, e] ^ there] += weight * blocks[own_list[0, e] ^ here]
        return 0

    def other(e, _):
        weight = other_list[2, e].astype(F32)
        right[other_list[0, e] ^ there] += weight * blocks[other_list[1, e] ^ here]
        return 0

    lax.fori_loop(0, own_list[3, 0], own, 0)
    lax.fori_loop(0, other_list[3, 0], other, 0)


def mixed(own_list, other_list, place, blocks):
    smem, vmem = pl.BlockSpec(memory_space=pltpu.SMEM), pl.BlockSpec(memory_space=pltpu.VMEM)
    shape = jax.ShapeDtypeStruct(blocks.shape, F32)
    return pl.pallas_call(
        mix_kernel,
        out_shape=(shape, shape),
        in_specs=[smem, smem, smem, vmem],
        out_specs=(vmem, vmem),
        cost_estimate=pl.CostEstimate(
            flops=blocks.size * 4, bytes_accessed=blocks.size * 12, transcendentals=0
        ),
        compiler_params=pltpu.CompilerParams(vmem_limit_bytes=VMEM),
        name="mix",
    )(own_list, other_list, place, blocks)


def finish_kernel(chunk, left, right, *refs):
    result, back = refs[-2:]
    block = (chunk[0, 0], chunk[0, 1])
    forth = product((left[0, 0], left[0, 1]), block)
    home = product(block, (right[0, 0], right[0, 1]))

    @pl.when(pl.program_id(0) == 0)
    def _():
        for part in range(2):
            if len(refs) == 4:
                result[part] = refs[0][part]
                back[part] = refs[1][part]
            else:
                result[part] = jnp.zeros_like(result[part])
                back[part] = jnp.zeros_like(back[part])

    for part in range(2):
        result[part] += forth[part]
        back[part] += home[part]


def finished(chunk, left, right, start, sums):
    size, width = chunk.shape[0], chunk.shape[-1]
    whole = (1, 2, width, width)
    total = pl.BlockSpec((2, width, width), lambda i: (0, 0, 0))
    shape = jax.ShapeDtypeStruct((2, width, width), F32)
    return pl.pallas_call(
        finish_kernel,
        out_shape=(shape, shape),
        grid=(size,),
        in_specs=[
            pl.BlockSpec(whole, lambda i: (i, 0, 0, 0)),
            pl.BlockSpec(whole, lambda i: (start + i, 0, 0, 0)),
            pl.BlockSpec(whole, lambda i: (start + i, 0, 0, 0)),
        ]
        + [total] * len(sums),
        out_specs=(total, total),
        cost_estimate=pl.CostEstimate(
            flops=size * 48 * width**3, bytes_accessed=size * 24 * width**2, transcendentals=0
        ),
        compiler_params=pltpu.CompilerParams(vmem_limit_bytes=VMEM),
        name="finish",
    )(chunk, left, right, *sums)


def back_kernel(low, size, chunk, right, back, out):
    real, imag = back[0, low : low + size], back[1, low : low + size]
    for k in range(chunk.shape[0]):
        more = product((chunk[k, 0], chunk[k, 1]), (right[k, 0], right[k, 1]))
        real += more[0]
        imag += more[1]
    out[0], out[1] = real, imag


def rows_back(chunk, right, start, back, low):
    size, _, rows, width = chunk.shape
    return pl.pallas_call(
        partial(back_kernel, low, rows),
        out_shape=jax.ShapeDtypeStruct((2, rows, width), F32),
        grid=(1,),
        in_specs=[
            pl.BlockSpec(chunk.shape, lambda i: (0, 0, 0, 0)),
            pl.BlockSpec((size, 2, width, width), lambda i: (start // size, 0, 0, 0)),
            pl.BlockSpec(back.shape, lambda i: (0, 0, 0)),
        ],
        out_specs=pl.BlockSpec((2, rows, width), lambda i: (0, 0, 0)),
        cost_estimate=pl.CostEstimate(
            flops=size * 24 * rows * width**2, bytes_accessed=12 * width**2, transcendentals=0
        ),
        compiler_params=pltpu.CompilerParams(vmem_limit_bytes=VMEM),
        name="rows_back",
    )(chunk, right, back)


def last_kernel(left, result, *refs):
    chunks, out = refs[:-1], refs[-1]
    real, imag = result[0], result[1]
    for k in range(left.shape[0]):
        block = tuple(jnp.concatenate([chunk[k, part] for chunk in chunks]) for part in range(2))
        more = product((left[k, 0], left[k, 1]), block)
        real += more[0]
        imag += more[1]
    out[0], out[1] = real, imag


def last_added(chunks, left, start, result):
    size, width = chunks[0].shape[0], chunks[0].shape[-1]
    return pl.pallas_call(
        last_kernel,
        out_shape=jax.ShapeDtypeStruct(result.shape, F32),
        grid=(1,),
        in_specs=[
            pl.BlockSpec((size, 2, width, width), lambda i: (start // size, 0, 0, 0)),
            pl.BlockSpec(result.shape, lambda i: (0, 0, 0)),
        ]
        + [pl.BlockSpec(chunk.shape, lambda i: (0, 0, 0, 0)) for chunk in chunks],
        out_specs=pl.BlockSpec(result.shape, lambda i: (0, 0, 0)),
        cost_estimate=pl.CostEstimate(
            flops=size * 24 * width**3, bytes_accessed=24 * width**2, transcendentals=0
        ),
        compiler_params=pltpu.CompilerParams(vmem_limit_bytes=VMEM),
        name="last",
    )(left, result, *chunks)


def body(meson, meson_src, peram, pair_left, pair_right, pair_weight, pair_count):
    axis = "sink"
    n = lax.axis_size(axis)
    sources, width = peram.shape[1], peram.shape[3]
    group, half = n // sources, n // 2
    me = lax.axis_index(axis)
    senders = [d for d in range(n) if (d & 1) == d // half]
    receivers = [d ^ half for d in senders]
    is_sender = (me & 1) == me // half
    mine = me // group

    def whole(shards):
        if group == 2:
            return shards, swapped(shards, axis, 1)
        for bit in range(group.bit_length() - 1):
            other = swapped(shards, axis, 1 << bit)
            upper = ((me >> bit) & 1) == 1
            low, high = jnp.where(upper, other, shards), jnp.where(upper, shards, other)
            shards = jnp.concatenate([low, high], axis=1)
        return shards[:, :width], shards[:, width:]

    odd = me & 1 if group == 2 else 0
    place = jnp.stack([mine, odd, mine ^ (sources // 2)]).astype(jnp.int32)
    count = jnp.broadcast_to(pair_count[:, None], pair_left.shape)
    own_list = jnp.concatenate([pair_left, pair_right, pair_weight, count])

    w0 = meson_src[None]
    w4 = swapped(w0, axis, half)
    s0 = whole(w0)
    w1 = swapped(w0, axis, group)
    other_list = swapped(own_list, axis, half)
    s1 = whole(w1)
    w23 = swapped(jnp.concatenate([w0, w1]), axis, 2 * group)
    s23 = whole(w23)
    w45 = jnp.concatenate([w4, swapped(w4, axis, group)])
    s45 = whole(w45)
    s67 = whole(swapped(w45, axis, 2 * group))

    lows = [sum(ROWS[:r]) * width // 256 for r in range(len(ROWS))]
    spans = [(low, rows * width // 256) for low, rows in zip(lows, ROWS, strict=True)]
    blocks, arrived, start = None, [], 0
    for name, source in zip(("0", "1", "23", "45"), (s0, s1, s23, s45), strict=True):
        (chunk,), blocks = blocks_of(place, meson, peram, *source, blocks, start, [(0, width)])
        arrived.append((name, start, sent(chunk, axis, half, senders)))
        start += source[0].shape[0]
    chunks, blocks = blocks_of(place, meson, peram, *s67, blocks, start, spans)
    chunks = [sent(chunk, axis, half, senders) for chunk in chunks]

    left, right = mixed(own_list, other_list, place, blocks)
    sums = ()
    for name, at, chunk in arrived:
        sums = finished(chunk, left, right, at, sums)
    result, back = sums
    returned = []
    for chunk, (low, _) in zip(chunks, spans, strict=True):
        rows = rows_back(chunk, right, start, back, low)
        returned.append(sent(rows, axis, half, receivers))
    result = last_added(chunks, left, start, result)
    return jnp.where(is_sender, jnp.concatenate(returned, axis=1), result)[None]


def solution(mesh):
    placed = (
        P(("grp", "sink"), None, None, None),
        P(("grp", "sink"), None),
        P(("grp", "sink"), None, None, None, None),
        P(("grp", "sink"), None),
        P(("grp", "sink"), None),
        P(("grp", "sink"), None),
        P(("grp", "sink")),
    )
    return jax.shard_map(
        body,
        mesh=mesh,
        in_specs=placed,
        out_specs=P(("grp", "sink"), None, None, None),
        check_vma=False,
    )
```
